1024 devices in a mesh: group: 16 (over z), expert: 64 (over x, y, core).
Axes of the slice: x: 4, y: 8, z: 16, core: 2. Of those that a mesh axis runs over, the one named last changes fastest.
Arguments:
- tokens: bfloat16 [16384, 3584], P(('group', 'expert')), parts along dimension 0, may hold values from -6 to 6
- w_in: bfloat16 [2, 3584, 131072], P(None, None, ('group', 'expert')), parts along dimension 2, may hold values from -0.09375 to 0.09375
- w_down: bfloat16 [131072, 3584], P(('group', 'expert')), parts along dimension 0, may hold values from -0.1875 to 0.1875
- old_place: int32 [128], P('group'), parts along dimension 0, may hold values from 0 to 5, as said below
- new_place: int32 [128], P('group'), parts along dimension 0, may hold values from 0 to 5, as said below
- expert_ids: int32 [16384, 2], P(('group', 'expert')), parts along dimension 0, may hold values from 0 to 5, all different within a row
- replica: int32 [16384, 2], P(('group', 'expert')), parts along dimension 0, may hold values from 0 to 1
- combine: float32 [16384, 2], P(('group', 'expert')), parts along dimension 0, may hold values from 0.2 to 1
Outputs:
- mixed: bfloat16 [16384, 3584], P(('group', 'expert')), parts along dimension 0
The draws below stay inside these ranges and needn't reach their ends.
There are 16 independent parts, one for each index of `group`. The reference program is written for one: setup_inputs(seed, part) draws one part's arguments, and reference() takes and returns one part's arrays. A program takes and returns all parts, laid end to end along the dimension named above; each array names one. Nothing has to cross between parts.
Inputs may be any that keep to these rules, and one draw needn't show every extreme that they name: Each of the 6 experts is held by one or two slots of old_place; exactly two experts are held twice. new_place is old_place with the entries of some pairs of slots 2 i and 2 i + 1 exchanged.
All inputs are finite; a program needn't handle non-finite values.
Results may differ from the reference program's by a relative error of at most 0.0057.
Values may be sent and summed in bfloat16 or wider, within the bound.
A program may use at most 32 MiB of HBM per device.

```python
import jax
import jax.numpy as jnp
from jax import lax

D = 3584
H_DEV = 128
SLOTS = 8
EXPERTS = 6
TOP = 2
CAP = 4
ROWS_DEV = 16
HID = 1024
ROWS = 1024
N_EXPERT = 64


def placements(key):
    key_first, key_second, key_order, key_flags, key_forced = jax.random.split(jax.random.fold_in(key, 11), 5)
    first = jax.random.randint(key_first, (), 0, EXPERTS)
    second = (first + jax.random.randint(key_second, (), 1, EXPERTS)) % EXPERTS
    pool_ids = jnp.concatenate([jnp.arange(EXPERTS, dtype=jnp.int32), jnp.stack([first, second]).astype(jnp.int32)])
    old_ids = pool_ids[jax.random.permutation(key_order, SLOTS)]
    swapped = jax.random.randint(key_flags, (SLOTS // 2,), 0, 2)
    forced = jax.random.randint(key_forced, (), 0, SLOTS // 2)
    swapped = swapped.at[forced].set(1)
    slot_ids = jnp.arange(SLOTS, dtype=jnp.int32)
    anchor = slot_ids + swapped[slot_ids // 2] * (1 - 2 * (slot_ids % 2))
    new_ids = old_ids[anchor]
    return (old_ids.astype(jnp.int32), new_ids.astype(jnp.int32))


def draw_old_place(key, part):
    return placements(key)[0]


def draw_new_place(key, part):
    return placements(key)[1]


def place_ends(result, key, smallest, high):
    spot = [jax.random.randint(jax.random.fold_in(key, axis), (), 0, length) for axis, length in enumerate(result.shape)]
    longest = result.shape.index(max(result.shape))
    beside = spot[:longest] + [(spot[longest] + 1) % result.shape[longest]] + spot[longest + 1:]
    return result.at[tuple(spot)].set(smallest).at[tuple(beside)].set(high)


def shard_levels(own_key, shape, cuts, smallest, largest):
    def one(axis_at, blocks):
        steps = jax.random.uniform(jax.random.fold_in(jax.random.fold_in(own_key, 6), axis_at), (blocks,), jnp.float32, smallest / len(cuts), largest / len(cuts))
        return jnp.repeat(jnp.exp(steps), shape[axis_at] // blocks).reshape((-1,) + (1,) * (len(shape) - axis_at - 1))

    factor_of = one(*cuts[0])
    for cut in cuts[1:]:
        factor_of = factor_of * one(*cut)
    return factor_of


def picks_of(own_key, rows, count, top, lift):
    ranking = jax.random.permutation(jax.random.fold_in(own_key, 1), count)
    favour = ranking
    for power in range(3):
        favour = favour * favour // count
    favour = favour * lift // count
    tickets = jax.random.randint(jax.random.fold_in(own_key, 2), (rows, count), 0, 4096) + favour
    fixed_rows = jax.random.permutation(jax.random.fold_in(own_key, 3), rows)[jnp.arange(count) % rows]
    tickets = jnp.where(jnp.arange(rows)[:, None] == fixed_rows[None, :], 1 << 14, tickets)
    priority = tickets * count + jnp.arange(count)
    return lax.top_k(priority.astype(jnp.int32), top)[1].astype(jnp.int32)


def noise(rng, dims, deviation, reach, cuts=(), held_as=jnp.bfloat16):
    array = jax.random.normal(rng, dims, jnp.float32) * deviation
    if len(cuts) > 0:
        array = shard_levels(rng, dims, cuts, -0.22, 0.18) * array
    return jnp.clip(array, min=-reach, max=reach).astype(held_as)


def setup_inputs(seed: int = 0, part: int = 0) -> dict:
    key_of = jax.random.split(jax.random.key(seed), 9)
    part_keys = jax.random.split(jax.random.fold_in(key_of[8], part), 9)
    return {
        "tokens": noise(part_keys[0], (ROWS, D), 1.0, 6.0, ((0, 64),)),
        "w_in": noise(part_keys[1], (2, D, SLOTS * HID), D ** -0.5, 0.09375, ((2, 64),)),
        "w_down": noise(part_keys[2], (SLOTS * HID, D), HID ** -0.5, 0.1875, ((0, 64),)),
        "old_place": draw_old_place(jax.random.fold_in(jax.random.fold_in(key_of[8], part), 71), part),
        "new_place": draw_new_place(jax.random.fold_in(jax.random.fold_in(key_of[8], part), 71), part),
        "expert_ids": picks_of(part_keys[5], ROWS, EXPERTS, TOP, 5461),
        "replica": place_ends(jax.random.randint(part_keys[6], (ROWS, TOP), 0, 2), jax.random.fold_in(part_keys[6], 1), 0, 1).astype(jnp.int32),
        "combine": jnp.clip(0.2 + 0.8 * jax.random.uniform(part_keys[7], (ROWS, TOP), jnp.float32) ** shard_levels(part_keys[7], (ROWS, TOP), ((0, 64),), -0.2, 0.2), 0.2, 1.0),
    }


def routing(new_place, expert_ids, replica):
    slot_ids = jnp.arange(SLOTS, dtype=jnp.int32)
    experts = jnp.arange(EXPERTS, dtype=jnp.int32)
    holders = (new_place[None, :] == experts[:, None]).astype(jnp.int32)
    counts = jnp.sum(holders, axis=1)
    before = jnp.cumsum(holders, axis=1) - holders
    expert_hot = (expert_ids[..., None] == experts).astype(jnp.int32)
    count_sel = jnp.sum(expert_hot * counts, axis=-1)
    wanted = replica % jnp.maximum(count_sel, 1)
    holder_sel = jnp.sum(expert_hot[..., None] * holders, axis=2)
    rank_sel = jnp.sum(expert_hot[..., None] * before, axis=2)
    chosen = holder_sel * (rank_sel == wanted[..., None]).astype(jnp.int32)
    return chosen, jnp.sum(chosen * slot_ids, axis=-1)


def reference(tokens, w_in, w_down, old_place, new_place, expert_ids, replica, combine):
    shards = N_EXPERT // SLOTS
    hid = H_DEV * shards
    slot_ids = jnp.arange(SLOTS, dtype=jnp.int32)
    source = jnp.where(new_place == old_place, slot_ids, slot_ids + 1 - 2 * (slot_ids % 2))
    chosen, dest_slot = routing(new_place, expert_ids, replica)
    per_dev = chosen.reshape(N_EXPERT, ROWS_DEV * TOP, SLOTS)
    position = (jnp.cumsum(per_dev, axis=1) - per_dev).reshape(ROWS, TOP, SLOTS)
    position = jnp.sum(chosen * position, axis=-1)
    is_kept = position < CAP
    device = (jnp.arange(ROWS, dtype=jnp.int32) // ROWS_DEV)[:, None]
    total = SLOTS * N_EXPERT * CAP
    target = jnp.where(is_kept, (dest_slot * N_EXPERT + device) * CAP + position, total).astype(jnp.int32)
    row_ids = jnp.broadcast_to(jnp.arange(ROWS, dtype=jnp.int32)[:, None], (ROWS, TOP))
    row_index = jnp.zeros((total + 1,), jnp.int32).at[target.reshape(-1)].set(row_ids.reshape(-1))
    filled = jnp.zeros((total + 1,), jnp.bfloat16).at[target.reshape(-1)].set(jnp.ones((ROWS * TOP,), jnp.bfloat16))
    gathered = tokens[row_index[:total]] * filled[:total, None]
    buffers = gathered.reshape(SLOTS, N_EXPERT * CAP, D)

    def slot_output(slot):
        start = (source[slot] * hid).astype(jnp.int32)
        slab_in = lax.dynamic_slice_in_dim(w_in, start, hid, 2)
        slab_down = lax.dynamic_slice_in_dim(w_down, start, hid, 0)
        rows_in = buffers[slot]
        gate = jnp.dot(rows_in, slab_in[0], preferred_element_type=jnp.float32)
        up = jnp.dot(rows_in, slab_in[1], preferred_element_type=jnp.float32)
        hidden = (jax.nn.silu(gate) * up).astype(jnp.bfloat16)
        pieces = jnp.einsum("rsh,shd->rsd", hidden.reshape(-1, shards, H_DEV).astype(jnp.float32),
                            slab_down.reshape(shards, H_DEV, D).astype(jnp.float32))
        pieces = lax.optimization_barrier(pieces.astype(jnp.bfloat16))
        return jnp.sum(pieces.astype(jnp.float32), axis=1)

    outputs = lax.map(slot_output, jnp.arange(SLOTS, dtype=jnp.int32))
    flat_out = jnp.concatenate([outputs.reshape(total, D), jnp.zeros((1, D), jnp.float32)], axis=0)
    picked = flat_out[target]
    mixed = jnp.sum(combine[..., None] * picked, axis=1)
    return mixed.astype(jnp.bfloat16)
```

```python
import functools

import jax
import jax.numpy as jnp
from jax import lax
from jax.experimental import pallas as pl
from jax.experimental.pallas import tpu as pltpu
from jax.sharding import PartitionSpec as P

SLOTS = 8
CAP = 4
NX, NY = 4, 8
META = 128
TILE = 512
F32 = jnp.float32
BF16 = jnp.bfloat16


def routing_meta(old_place, new_place, expert_ids, replica, combine):
    rows = expert_ids.shape[0]
    lane = lax.broadcasted_iota(jnp.int32, (1, META), 1)
    new_vec = jnp.full((1, META), -1, jnp.int32)
    old_vec = jnp.full((1, META), -1, jnp.int32)
    for t in range(SLOTS):
        new_vec = jnp.where(lane == t, new_place[t], new_vec)
        old_vec = jnp.where(lane == t, old_place[t], old_vec)
    count = jnp.zeros((1, META), jnp.int32)
    rank = jnp.zeros((1, META), jnp.int32)
    for t in range(SLOTS):
        same = jnp.where(new_vec == new_place[t], 1, 0)
        count = count + same
        rank = rank + jnp.where(lane > t, same, 0)
    source = jnp.where(new_vec == old_vec, lane, lane + 1 - 2 * (lane & 1))
    chosen = []
    for k in range(2):
        wanted = replica[:, k:k + 1]
        wanted = jnp.where(wanted < count, wanted, wanted - count)
        hit = (new_vec == expert_ids[:, k:k + 1]) & (rank == wanted)
        chosen.append(jnp.where(hit, 1.0, 0.0))
    row_i = lax.broadcasted_iota(jnp.int32, (rows, rows), 0)
    col_i = lax.broadcasted_iota(jnp.int32, (rows, rows), 1)
    earlier = jnp.where(col_i < row_i, 1.0, 0.0).astype(BF16)
    before = jnp.dot(earlier, (chosen[0] + chosen[1]).astype(BF16), preferred_element_type=F32)
    lanes = lax.broadcasted_iota(jnp.int32, (rows, META), 1)
    column = (lanes & 31).astype(F32)
    block = lanes >> 5
    source_f = (source * CAP).astype(F32)
    meta = jnp.zeros((rows, META), F32)
    for k in range(2):
        ahead = before if k == 0 else before + chosen[0]
        position = jnp.sum(chosen[k] * ahead, axis=1, keepdims=True)
        target = jnp.sum(chosen[k] * source_f, axis=1, keepdims=True) + position
        weight = combine[:, k:k + 1]
        high = weight.astype(BF16).astype(F32)
        middle = (weight - high).astype(BF16).astype(F32)
        low = weight - high - middle
        value = jnp.where(block == 0, high, jnp.where(block == 1, middle, jnp.where(block == 2, low, 1.0)))
        meta = meta + jnp.where((column == target) & (position < float(CAP)), value, 0.0)
    return meta.astype(BF16)


def kernel(tokens, w_in, w_down, old_place, new_place, expert_ids, replica, combine, out,
           units, sel, rows, w_gu, w_d, p_send, p_recv, p_own, r_send, r_recv, part, y_send, y_recv,
           ssem, rsem, wsem):
    width = tokens.shape[1]
    hid = w_down.shape[0]
    me = lax.axis_index("expert")
    core = me % 2
    y = (me // 2) % NY
    x = me // (2 * NY)
    half = y // (NY // 2)

    def device(xx, yy, cc):
        return {"expert": (xx * NY + yy) * 2 + cc}

    up = device(x, (y + 1) % NY, core)
    down = device(x, (y + NY - 1) % NY, core)
    partner = device(x, y, 1 - core)
    right = [device((x + d) % NX, y, core) for d in range(NX)]
    left = [device((x + NX - d) % NX, y, core) for d in range(NX)]

    barrier = pltpu.get_barrier_semaphore()
    peers = [up, down, partner] + right[1:]
    for peer in peers:
        pl.semaphore_signal(barrier, inc=1, device_id=peer, device_id_type=pl.DeviceIdType.MESH)

    loads = [
        pltpu.make_async_copy(w_in.at[0], w_gu.at[:, 0:hid], wsem.at[0]),
        pltpu.make_async_copy(w_in.at[1], w_gu.at[:, hid:2 * hid], wsem.at[1]),
        pltpu.make_async_copy(w_down, w_d, wsem.at[2]),
    ]
    for load in loads:
        load.start()

    units[0, :, META:] = tokens[...]
    units[0, :, :META] = routing_meta(old_place, new_place, expert_ids[...], replica[...], combine[...])
    pl.semaphore_wait(barrier, len(peers))

    sent = []

    def push(src, dst, target):
        i = len(sent)
        copy = pltpu.make_async_remote_copy(
            src_ref=src, dst_ref=dst, send_sem=ssem.at[i], recv_sem=rsem.at[i],
            device_id=target, device_id_type=pl.DeviceIdType.MESH)
        copy.start()
        sent.append(copy)
        return copy

    cuts = (pl.ds(0, 1920), pl.ds(1920, 1792))

    def forward(src, dst, target, c):
        return push(units.at[src, :, cuts[c]], units.at[dst, :, cuts[c]], target)

    a1 = [(forward(0, 1, up, c), forward(0, 2, down, c)) for c in range(2)]
    a2 = []
    for c in range(2):
        a1[c][0].wait_recv()
        u = forward(1, 3, up, c)
        a1[c][1].wait_recv()
        a2.append((u, forward(2, 4, down, c)))
    a3 = []
    for c in range(2):
        a2[c][0].wait_recv()
        u = forward(3, 5, up, c)
        a2[c][1].wait_recv()
        a3.append((u, forward(4, 6, down, c)))

    lane_i = lax.broadcasted_iota(jnp.int32, (META, 4 * META), 0)
    n_i = lax.broadcasted_iota(jnp.int32, (META, 4 * META), 1)
    n_in = n_i & (META - 1)
    wanted = 32 * (n_i >> 7) + 8 * ((x + (n_in >> 4)) & (NX - 1)) + CAP * half + (n_in & 3)
    spread = jnp.where((lane_i == wanted) & (n_in < 64), 1.0, 0.0).astype(BF16)
    u_row = lax.broadcasted_iota(jnp.int32, (64, 64), 0) >> 4
    u_col = (lax.broadcasted_iota(jnp.int32, (64, 64), 1) >> 2) & 3
    same_unit = u_row == u_col

    def select(g):
        meta = units[4 * g:4 * g + 4, :, :META].reshape(64, META)
        picks = jnp.dot(meta, spread, preferred_element_type=F32)
        mats = [jnp.where(same_unit, picks[:, q * META:q * META + 64], 0.0).astype(BF16) for q in range(4)]
        for j in range(width // TILE):
            group = units[4 * g:4 * g + 4, :, META + j * TILE:META + (j + 1) * TILE].reshape(64, TILE)
            got = lax.dot_general(mats[3], group, (((0,), (0,)), ((), ())), preferred_element_type=F32)
            got = got.astype(BF16)
            rows[g, 0, 0, :, j * TILE:(j + 1) * TILE] = got[0:16]
            for d in range(1, NX):
                sel[g, d, :, j * TILE:(j + 1) * TILE] = got[16 * d:16 * d + 16]
        weights = jnp.concatenate(mats[:3], axis=0)
        copies = [None] + [push(sel.at[g, d], rows.at[g, 0, d], right[d]) for d in range(1, NX)]
        return weights, copies

    def swap(g, d):
        return push(rows.at[g, 0, d], rows.at[g, 1, d], partner)

    def experts(g):
        block = rows[g].reshape(2 * 64, width)
        gate_up = jnp.dot(block, w_gu[...], preferred_element_type=F32)
        gate = gate_up[:, :hid]
        hidden = (gate * jax.nn.sigmoid(gate) * gate_up[:, hid:]).astype(BF16)
        for j in range(width // TILE):
            cut = slice(j * TILE, (j + 1) * TILE)
            value = jnp.dot(hidden, w_d[:, cut], preferred_element_type=F32)
            p_own[g, :, cut] = value[:64]
            p_send[g, :, cut] = value[64:].astype(BF16)
        return push(p_send.at[g], p_recv.at[g], partner)

    def give_back(g, copy):
        copy.wait_recv()
        for d in range(NX):
            total = p_own[g, 16 * d:16 * d + 16] + p_recv[g, 16 * d:16 * d + 16].astype(F32)
            if d == 0:
                r_recv[g, 0:16] = total.astype(BF16)
            else:
                r_send[g, 16 * d:16 * d + 16] = total.astype(BF16)
        return [push(r_send.at[g, pl.ds(16 * d, 16)], r_recv.at[g, pl.ds(16 * d, 16)], left[d])
                for d in range(1, NX)]

    def mix(g, weights, copies):
        for copy in copies:
            copy.wait_recv()
        for j in range(width // TILE):
            cut = slice(j * TILE, (j + 1) * TILE)
            value = jnp.dot(weights, r_recv[g, :, cut], preferred_element_type=F32)
            value = value[0:64] + value[64:128] + value[128:192]
            part[4 * g:4 * g + 4, :, cut] = value.reshape(4, 16, TILE)

    weights_a, x_a = select(0)
    a4 = []
    for c in range(2):
        a3[c][0].wait_recv()
        if c == 0:
            a4.append(forward(5, 7, up, 0))
        a3[c][1].wait_recv()
        if c == 1:
            a4.append(forward(6, 7, down, 1))
    s_a = [swap(0, 0)]
    for copy in a4:
        copy.wait_recv()
    weights_b, x_b = select(1)
    s_b = [swap(1, 0)]
    for d in range(1, NX):
        x_a[d].wait_recv()
        s_a.append(swap(0, d))
    for load in loads:
        load.wait()
    for copy in s_a:
        copy.wait_recv()
    p_a = experts(0)
    for d in range(1, NX):
        x_b[d].wait_recv()
        s_b.append(swap(1, d))
    r_a = give_back(0, p_a)
    for copy in s_b:
        copy.wait_recv()
    p_b = experts(1)
    r_b = give_back(1, p_b)
    mix(0, weights_a, r_a)
    mix(1, weights_b, r_b)

    halves = (slice(0, width // 2), slice(width // 2, width))

    def hand(k, dst, c, target, arrived):
        value = part[k, :, halves[c]]
        if arrived is not None:
            arrived.wait_recv()
            value = value + y_recv[k, :, halves[c]].astype(F32)
        y_send[k, :, halves[c]] = value.astype(BF16)
        cut = pl.ds(c * (width // 2), width // 2)
        return push(y_send.at[k, :, cut], y_recv.at[dst, :, cut], target)

    got_down = {0: hand(7, 5, 0, down, None), 1: None}
    got_up = {0: None, 1: hand(7, 6, 1, up, None)}
    for k_down, d_down, k_up, d_up in ((5, 3, 6, 4), (3, 1, 4, 2), (1, 0, 2, 7)):
        next_down, next_up = {}, {}
        for c in range(2):
            order = (1 - c) if k_down == 5 else c
            next_down[order] = hand(k_down, d_down, order, down, got_down[order])
            other = c
            next_up[other] = hand(k_up, d_up, other, up, got_up[other])
        got_down, got_up = next_down, next_up
    for c in range(2):
        got_down[c].wait_recv()
        got_up[c].wait_recv()
        value = (part[0, :, halves[c]] + y_recv[0, :, halves[c]].astype(F32)
                 + y_recv[7, :, halves[c]].astype(F32))
        out[:, halves[c]] = value.astype(BF16)
    for copy in sent:
        copy.wait_send()


COPIES = 14 + 6 + 8 + 2 + 6 + 14


def body(tokens, w_in, w_down, old_place, new_place, expert_ids, replica, combine):
    count, width = tokens.shape
    hid = w_down.shape[0]
    vmem = pl.BlockSpec(memory_space=pltpu.VMEM)
    smem = pl.BlockSpec(memory_space=pltpu.SMEM)
    hbm = pl.BlockSpec(memory_space=pl.ANY)
    return pl.pallas_call(
        kernel,
        out_shape=jax.ShapeDtypeStruct((count, width), BF16),
        in_specs=[vmem, hbm, hbm, smem, smem, vmem, vmem, vmem],
        out_specs=vmem,
        scratch_shapes=[
            pltpu.VMEM((8, count, META + width), BF16),
            pltpu.VMEM((2, NX, 16, width), BF16),
            pltpu.VMEM((2, 2, NX, 16, width), BF16),
            pltpu.VMEM((width, 2 * hid), BF16),
            pltpu.VMEM((hid, width), BF16),
            pltpu.VMEM((2, 64, width), BF16),
            pltpu.VMEM((2, 64, width), BF16),
            pltpu.VMEM((2, 64, width), F32),
            pltpu.VMEM((2, 64, width), BF16),
            pltpu.VMEM((2, 64, width), BF16),
            pltpu.VMEM((8, count, width), F32),
            pltpu.VMEM((8, count, width), BF16),
            pltpu.VMEM((8, count, width), BF16),
            pltpu.SemaphoreType.DMA((COPIES,)),
            pltpu.SemaphoreType.DMA((COPIES,)),
            pltpu.SemaphoreType.DMA((3,)),
        ],
        compiler_params=pltpu.CompilerParams(collective_id=0, has_side_effects=True),
    )(tokens, w_in, w_down, old_place, new_place, expert_ids, replica, combine)


def solution(mesh):
    placed = (
        P(("group", "expert"), None),
        P(None, None, ("group", "expert")),
        P(("group", "expert"), None),
        P("group"),
        P("group"),
        P(("group", "expert"), None),
        P(("group", "expert"), None),
        P(("group", "expert"), None),
    )
    return jax.shard_map(
        body, mesh=mesh, in_specs=placed, out_specs=P(("group", "expert"), None), check_vma=False
    )
```

```python
import jax
import jax.numpy as jnp
from jax import lax
from jax.experimental import pallas as pl
from jax.experimental.pallas import tpu as pltpu
from jax.sharding import PartitionSpec as P

SLOTS = 8
CAP = 4
NX, NY = 4, 8
META = 128
TILE = 512
F32 = jnp.float32
BF16 = jnp.bfloat16


def routing_meta(old_place, new_place, expert_ids, replica, combine):
    rows = expert_ids.shape[1]
    diagonal = (lax.broadcasted_iota(jnp.int32, (rows, rows), 0)
                == lax.broadcasted_iota(jnp.int32, (rows, rows), 1))

    def column_of(array, k):
        return jnp.sum(jnp.where(diagonal, array[k:k + 1, :], 0), axis=1, keepdims=True)

    lane = lax.broadcasted_iota(jnp.int32, (1, META), 1)
    new_vec = jnp.full((1, META), -1, jnp.int32)
    old_vec = jnp.full((1, META), -1, jnp.int32)
    for t in range(SLOTS):
        new_vec = jnp.where(lane == t, new_place[t], new_vec)
        old_vec = jnp.where(lane == t, old_place[t], old_vec)
    count = jnp.zeros((1, META), jnp.int32)
    rank = jnp.zeros((1, META), jnp.int32)
    for t in range(SLOTS):
        same = jnp.where(new_vec == new_place[t], 1, 0)
        count = count + same
        rank = rank + jnp.where(lane > t, same, 0)
    source = jnp.where(new_vec == old_vec, lane, lane + 1 - 2 * (lane & 1))
    chosen = []
    for k in range(2):
        wanted = column_of(replica, k)
        wanted = jnp.where(wanted < count, wanted, wanted - count)
        hit = (new_vec == column_of(expert_ids, k)) & (rank == wanted)
        chosen.append(jnp.where(hit, 1.0, 0.0))
    row_i = lax.broadcasted_iota(jnp.int32, (rows, rows), 0)
    col_i = lax.broadcasted_iota(jnp.int32, (rows, rows), 1)
    earlier = jnp.where(col_i < row_i, 1.0, 0.0).astype(BF16)
    before = jnp.dot(earlier, (chosen[0] + chosen[1]).astype(BF16), preferred_element_type=F32)
    lanes = lax.broadcasted_iota(jnp.int32, (rows, META), 1)
    column = (lanes & 31).astype(F32)
    block = lanes >> 5
    source_f = (source * CAP).astype(F32)
    meta = jnp.zeros((rows, META), F32)
    for k in range(2):
        ahead = before if k == 0 else before + chosen[0]
        position = jnp.sum(chosen[k] * ahead, axis=1, keepdims=True)
        target = jnp.sum(chosen[k] * source_f, axis=1, keepdims=True) + position
        weight = column_of(combine, k)
        high = weight.astype(BF16).astype(F32)
        middle = (weight - high).astype(BF16).astype(F32)
        low = weight - high - middle
        value = jnp.where(block == 0, high, jnp.where(block == 1, middle, jnp.where(block == 2, low, 1.0)))
        meta = meta + jnp.where((column == target) & (position < float(CAP)), value, 0.0)
    return meta.astype(BF16)


def kernel(tokens, w_in, w_down, old_place, new_place, expert_ids, replica, combine, out,
           units, sel, rows, w_gu, w_d, r_send, r_recv, part, y_send, y_recv, y_far,
           old_s, new_s, ids_v, rep_v, comb_v, ssem, rsem, wsem):
    width = tokens.shape[1]
    hid = w_down.shape[0]
    me = lax.axis_index("expert")
    core = me % 2
    y = (me // 2) % NY
    x = me // (2 * NY)
    half = y // (NY // 2)

    def device(xx, yy, cc):
        return {"expert": (xx * NY + yy) * 2 + cc}

    up, up2 = device(x, (y + 1) % NY, core), device(x, (y + 2) % NY, core)
    down, down2 = device(x, (y + NY - 1) % NY, core), device(x, (y + NY - 2) % NY, core)
    partner = device(x, y, 1 - core)
    right = [device((x + d) % NX, y, core) for d in range(NX)]
    left = [device((x + NX - d) % NX, y, core) for d in range(NX)]

    barrier = pltpu.get_barrier_semaphore()
    peers = [up, down, up2, down2, partner] + right[1:]
    for peer in peers:
        pl.semaphore_signal(barrier, inc=1, device_id=peer, device_id_type=pl.DeviceIdType.MESH)

    split = width // 2
    quarter = width // 4

    def local(i, src, dst):
        copy = pltpu.make_async_copy(src, dst, wsem.at[i])
        copy.start()
        return copy

    small = [local(i, src, dst) for i, (src, dst) in enumerate((
        (old_place, old_s), (new_place, new_s), (expert_ids, ids_v), (replica, rep_v), (combine, comb_v)))]
    own = [local(5, tokens.at[:, pl.ds(0, split)], units.at[0, :, pl.ds(0, split)]),
           local(6, tokens.at[:, pl.ds(split, split)], units.at[0, :, pl.ds(split + META, split)])]
    loads = [local(7, w_in.at[0], w_gu.at[:, 0:hid]), local(8, w_in.at[1], w_gu.at[:, 2 * hid:3 * hid]),
             local(9, w_down, w_d.at[0:hid])]

    sent = []

    def push(src, dst, target):
        i = len(sent)
        copy = pltpu.make_async_remote_copy(
            src_ref=src, dst_ref=dst, send_sem=ssem.at[i], recv_sem=rsem.at[i],
            device_id=target, device_id_type=pl.DeviceIdType.MESH)
        copy.start()
        sent.append(copy)
        return copy

    cuts = (pl.ds(0, quarter), pl.ds(quarter, quarter), pl.ds(split, META + quarter),
            pl.ds(split + META + quarter, quarter))
    parts = (slice(0, split), slice(split, width))
    places = (slice(0, split), slice(split + META, META + width))
    spots = slice(split, split + META)
    quarters = [slice(c * quarter, (c + 1) * quarter) for c in range(4)]
    cut_q = [pl.ds(c * quarter, quarter) for c in range(4)]
    cut_h = [pl.ds(h * split, split) for h in range(2)]

    def forward(src, dst, target, c):
        return push(units.at[src, :, cuts[c]], units.at[dst, :, cuts[c]], target)

    pl.semaphore_wait(barrier, len(peers))
    a1 = {}
    for c in (0, 1):
        piece = tokens.at[:, cut_q[c]]
        a1[c] = (push(piece, units.at[1, :, cuts[c]], up), push(piece, units.at[2, :, cuts[c]], down))
    w_peer = [push(w_in.at[0], w_gu.at[:, hid:2 * hid], partner),
              push(w_in.at[1], w_gu.at[:, 3 * hid:4 * hid], partner),
              push(w_down, w_d.at[hid:2 * hid], partner)]
    for copy in small:
        copy.wait()
    units[0, :, spots] = routing_meta(old_s, new_s, ids_v[...], rep_v[...], comb_v[...])
    own[1].wait()
    a1[2] = (forward(0, 1, up, 2), forward(0, 2, down, 2))
    piece = tokens.at[:, cut_q[3]]
    a1[3] = (push(piece, units.at[1, :, cuts[3]], up), push(piece, units.at[2, :, cuts[3]], down))
    a2 = []
    for c in range(4):
        a1[c][0].wait_recv()
        u = forward(1, 3, up, c)
        a1[c][1].wait_recv()
        a2.append((u, forward(2, 4, down, c)))
    a3, a4 = [], []
    for c in range(4):
        a2[c][0].wait_recv()
        u = forward(3, 5, up, c)
        if c % 2 == 0:
            a4.append(forward(3, 7, up2, c))
        a2[c][1].wait_recv()
        a3.append((u, forward(4, 6, down, c)))
        if c % 2 == 1:
            a4.append(forward(4, 7, down2, c))

    def wanted_by(n, block):
        return 32 * block + 8 * ((x + (n >> 4)) & (NX - 1)) + CAP * half + (n & 3)

    lane_i = lax.broadcasted_iota(jnp.int32, (META, 3 * META), 0)
    n_i = lax.broadcasted_iota(jnp.int32, (META, 3 * META), 1)
    n_in = n_i & (META - 1)
    spread = jnp.where((lane_i == wanted_by(n_in, n_i >> 7)) & (n_in < 64), 1.0, 0.0).astype(BF16)
    n_t = lax.broadcasted_iota(jnp.int32, (64, META), 0)
    spread_t = jnp.where(lax.broadcasted_iota(jnp.int32, (64, META), 1) == wanted_by(n_t, 3), 1.0, 0.0).astype(BF16)
    i_row = lax.broadcasted_iota(jnp.int32, (64, 64), 0)
    i_col = lax.broadcasted_iota(jnp.int32, (64, 64), 1)
    same_unit = (i_row >> 4) == ((i_col >> 2) & 3)
    same_unit_t = (i_col >> 4) == ((i_row >> 2) & 3)

    def weights_of(g):
        meta = units[4 * g:4 * g + 4, :, spots].reshape(64, META)
        picks = jnp.dot(meta, spread, preferred_element_type=F32)
        return jnp.concatenate(
            [jnp.where(same_unit, picks[:, q * META:q * META + 64], 0.0).astype(BF16) for q in range(3)], axis=0)

    def select(g):
        meta = units[4 * g:4 * g + 4, :, spots].reshape(64, META)
        picks = lax.dot_general(spread_t, meta, (((1,), (1,)), ((), ())), preferred_element_type=F32)
        picks = jnp.where(same_unit_t, picks, 0.0).astype(BF16)
        copies = []
        for h in range(2):
            for j in range(7):
                at = h * (split + META) + j * 256
                cut = slice(h * split + j * 256, h * split + (j + 1) * 256)
                group = units[4 * g:4 * g + 4, :, at:at + 256].reshape(64, 256)
                got = jnp.dot(picks, group, preferred_element_type=F32)
                got = got.astype(BF16)
                rows[g, 0, :, cut] = got[0:16]
                for d in range(1, NX):
                    sel[g, d, :, cut] = got[16 * d:16 * d + 16]
            copies.append({d: push(sel.at[g, d, :, cut_h[h]], rows.at[g, d, :, cut_h[h]], right[d])
                           for d in (2, 1, 3)})
        return copies

    def experts(g, copies):
        gate_up = jnp.zeros((64, 4 * hid), F32)
        for h in range(2):
            for d in (1, 3, 2):
                copies[h][d].wait_recv()
            block = rows[g, :, :, parts[h]].reshape(64, split)
            gate_up = gate_up + jnp.dot(block, w_gu[parts[h], :], preferred_element_type=F32)
        gate = gate_up[:, :2 * hid]
        hidden = (gate * jax.nn.sigmoid(gate) * gate_up[:, 2 * hid:]).astype(BF16)
        back = []
        for h in range(2):
            for j in range(7):
                cut = slice(h * split + j * 256, h * split + (j + 1) * 256)
                value = jnp.dot(hidden, w_d[:, cut], preferred_element_type=F32).astype(BF16)
                r_recv[g, 0:16, cut] = value[0:16]
                r_send[g, 16:64, cut] = value[16:64]
            back.append([push(r_send.at[g, pl.ds(16 * d, 16), cut_h[h]], r_recv.at[g, pl.ds(16 * d, 16), cut_h[h]],
                              left[d]) for d in (2, 1, 3)])
        return back

    def mix(g, h, weights, copies):
        for copy in copies:
            copy.wait_recv()
        for j in range(7):
            cut = slice(h * split + j * 256, h * split + (j + 1) * 256)
            value = jnp.dot(weights, r_recv[g, :, cut], preferred_element_type=F32)
            value = value[0:64] + value[64:128] + value[128:192]
            part[4 * g:4 * g + 4, :, cut] = value.reshape(4, 16, 256)

    def hand(k, dst, c, target, *arrived):
        value = part[k, :, quarters[c]]
        for copy, buffer in arrived:
            copy.wait_recv()
            value = value + buffer[:, quarters[c]].astype(F32)
        y_send[k, :, quarters[c]] = value.astype(BF16)
        return push(y_send.at[k, :, cut_q[c]], dst.at[:, cut_q[c]], target)

    own[0].wait()
    x_a = select(0)
    for c in range(4):
        a3[c][0].wait_recv()
        a3[c][1].wait_recv()
    for copy in a4:
        copy.wait_recv()
    x_b = select(1)
    for load in loads:
        load.wait()
    for copy in w_peer:
        copy.wait_recv()
    r_a = experts(0, x_a)
    r_b = experts(1, x_b)
    weights_a, weights_b = weights_of(0), weights_of(1)
    for h in range(2):
        mix(0, h, weights_a, r_a[h])
    far_down, far_up, go_down, go_up = {}, {}, {}, {}
    for h in range(2):
        mix(1, h, weights_b, r_b[h])
        even, odd = 2 * h, 2 * h + 1
        far_down[even] = hand(7, y_far.at[0], even, down2)
        far_up[odd] = hand(7, y_far.at[1], odd, up2)
        for c in (odd, even):
            go_down[c] = hand(5, y_recv.at[3], c, down)
        for c in (even, odd):
            go_up[c] = hand(6, y_recv.at[4], c, up)
    order = ((1, 0), (3, 2), (0, 1), (2, 3))
    for c_down, c_up in order:
        extra = ((far_down[c_down], y_far.at[0]),) if c_down in far_down else ()
        go_down[c_down] = hand(3, y_recv.at[1], c_down, down, (go_down[c_down], y_recv.at[3]), *extra)
        extra = ((far_up[c_up], y_far.at[1]),) if c_up in far_up else ()
        go_up[c_up] = hand(4, y_recv.at[2], c_up, up, (go_up[c_up], y_recv.at[4]), *extra)
    for c_down, c_up in order:
        go_down[c_down] = hand(1, y_recv.at[0], c_down, down, (go_down[c_down], y_recv.at[1]))
        go_up[c_up] = hand(2, y_recv.at[7], c_up, up, (go_up[c_up], y_recv.at[2]))
    for c in (1, 3, 0, 2):
        go_down[c].wait_recv()
        go_up[c].wait_recv()
        value = (part[0, :, quarters[c]] + y_recv[0, :, quarters[c]].astype(F32)
                 + y_recv[7, :, quarters[c]].astype(F32))
        out[:, quarters[c]] = value.astype(BF16)
    for copy in sent:
        copy.wait_send()


COPIES = 28 + 3 + 12 + 12 + 28


def body(tokens, w_in, w_down, old_place, new_place, expert_ids, replica, combine):
    count, width = tokens.shape
    hid = w_down.shape[0]
    vmem = pl.BlockSpec(memory_space=pltpu.VMEM)
    hbm = pl.BlockSpec(memory_space=pl.ANY)
    return pl.pallas_call(
        kernel,
        out_shape=jax.ShapeDtypeStruct((count, width), BF16),
        in_specs=[hbm] * 8,
        out_specs=vmem,
        scratch_shapes=[
            pltpu.VMEM((8, count, META + width), BF16),
            pltpu.VMEM((2, NX, 16, width), BF16),
            pltpu.VMEM((2, NX, 16, width), BF16),
            pltpu.VMEM((width, 4 * hid), BF16),
            pltpu.VMEM((2 * hid, width), BF16),
            pltpu.VMEM((2, 64, width), BF16),
            pltpu.VMEM((2, 64, width), BF16),
            pltpu.VMEM((8, count, width), F32),
            pltpu.VMEM((8, count, width), BF16),
            pltpu.VMEM((8, count, width), BF16),
            pltpu.VMEM((2, count, width), BF16),
            pltpu.SMEM((SLOTS,), jnp.int32),
            pltpu.SMEM((SLOTS,), jnp.int32),
            pltpu.VMEM((2, count), jnp.int32),
            pltpu.VMEM((2, count), jnp.int32),
            pltpu.VMEM((2, count), F32),
            pltpu.SemaphoreType.DMA((COPIES,)),
            pltpu.SemaphoreType.DMA((COPIES,)),
            pltpu.SemaphoreType.DMA((10,)),
        ],
        compiler_params=pltpu.CompilerParams(collective_id=0, has_side_effects=True),
    )(tokens, w_in, w_down, old_place, new_place, expert_ids.T, replica.T, combine.T)


def solution(mesh):
    placed = (
        P(("group", "expert"), None),
        P(None, None, ("group", "expert")),
        P(("group", "expert"), None),
        P("group"),
        P("group"),
        P(("group", "expert"), None),
        P(("group", "expert"), None),
        P(("group", "expert"), None),
    )
    return jax.shard_map(
        body, mesh=mesh, in_specs=placed, out_specs=P(("group", "expert"), None), check_vma=False
    )
```

```python
import jax
import jax.numpy as jnp
from jax import lax
from jax.experimental import pallas as pl
from jax.experimental.pallas import tpu as pltpu
from jax.sharding import PartitionSpec as P

SLOTS = 8
CAP = 4
NX, NY = 4, 8
META = 128
TILE = 512
F32 = jnp.float32
BF16 = jnp.bfloat16


def routing_meta(old_place, new_place, expert_ids, replica, combine):
    rows = expert_ids.shape[1]
    diagonal = (lax.broadcasted_iota(jnp.int32, (rows, rows), 0)
                == lax.broadcasted_iota(jnp.int32, (rows, rows), 1))

    def column_of(array, k):
        return jnp.sum(jnp.where(diagonal, array[k:k + 1, :], 0), axis=1, keepdims=True)

    lane = lax.broadcasted_iota(jnp.int32, (1, META), 1)
    new_vec = jnp.full((1, META), -1, jnp.int32)
    old_vec = jnp.full((1, META), -1, jnp.int32)
    for t in range(SLOTS):
        new_vec = jnp.where(lane == t, new_place[t], new_vec)
        old_vec = jnp.where(lane == t, old_place[t], old_vec)
    count = jnp.zeros((1, META), jnp.int32)
    rank = jnp.zeros((1, META), jnp.int32)
    for t in range(SLOTS):
        same = jnp.where(new_vec == new_place[t], 1, 0)
        count = count + same
        rank = rank + jnp.where(lane > t, same, 0)
    source = jnp.where(new_vec == old_vec, lane, lane + 1 - 2 * (lane & 1))
    chosen = []
    for k in range(2):
        wanted = column_of(replica, k)
        wanted = jnp.where(wanted < count, wanted, wanted - count)
        hit = (new_vec == column_of(expert_ids, k)) & (rank == wanted)
        chosen.append(jnp.where(hit, 1.0, 0.0))
    row_i = lax.broadcasted_iota(jnp.int32, (rows, rows), 0)
    col_i = lax.broadcasted_iota(jnp.int32, (rows, rows), 1)
    earlier = jnp.where(col_i < row_i, 1.0, 0.0).astype(BF16)
    before = jnp.dot(earlier, (chosen[0] + chosen[1]).astype(BF16), preferred_element_type=F32)
    lanes = lax.broadcasted_iota(jnp.int32, (rows, META), 1)
    column = (lanes & 31).astype(F32)
    block = lanes >> 5
    source_f = (source * CAP).astype(F32)
    meta = jnp.zeros((rows, META), F32)
    for k in range(2):
        ahead = before if k == 0 else before + chosen[0]
        position = jnp.sum(chosen[k] * ahead, axis=1, keepdims=True)
        target = jnp.sum(chosen[k] * source_f, axis=1, keepdims=True) + position
        weight = column_of(combine, k)
        high = weight.astype(BF16).astype(F32)
        middle = (weight - high).astype(BF16).astype(F32)
        low = weight - high - middle
        value = jnp.where(block == 0, high, jnp.where(block == 1, middle, jnp.where(block == 2, low, 1.0)))
        meta = meta + jnp.where((column == target) & (position < float(CAP)), value, 0.0)
    return meta.astype(BF16)


def kernel(tokens, w_in, w_down, old_place, new_place, expert_ids, replica, combine, out,
           units, sel, rows, w_gu, w_d, r_send, r_recv, part, y_send, y_recv, y_far,
           old_s, new_s, ids_v, rep_v, comb_v, out_v, ssem, rsem, wsem):
    width = tokens.shape[1]
    hid = w_down.shape[0]
    me = lax.axis_index("expert")
    core = me % 2
    y = (me // 2) % NY
    x = me // (2 * NY)
    half = y // (NY // 2)

    def device(xx, yy, cc):
        return {"expert": (xx * NY + yy) * 2 + cc}

    up, up2 = device(x, (y + 1) % NY, core), device(x, (y + 2) % NY, core)
    down, down2 = device(x, (y + NY - 1) % NY, core), device(x, (y + NY - 2) % NY, core)
    partner = device(x, y, 1 - core)
    right = [device((x + d) % NX, y, core) for d in range(NX)]
    left = [device((x + NX - d) % NX, y, core) for d in range(NX)]

    barrier = pltpu.get_barrier_semaphore()
    peers = [up, down, up2, down2, partner] + right[1:]
    for peer in peers:
        pl.semaphore_signal(barrier, inc=1, device_id=peer, device_id_type=pl.DeviceIdType.MESH)

    split = width // 2
    quarter = width // 4

    def local(i, src, dst):
        copy = pltpu.make_async_copy(src, dst, wsem.at[i])
        copy.start()
        return copy

    small = [local(i, src, dst) for i, (src, dst) in enumerate((
        (old_place, old_s), (new_place, new_s), (expert_ids, ids_v), (replica, rep_v), (combine, comb_v)))]
    own = local(5, tokens, units.at[0, :, pl.ds(META, width)])
    loads = [local(6, w_in.at[0], w_gu.at[:, 0:hid]), local(7, w_in.at[1], w_gu.at[:, 2 * hid:3 * hid]),
             local(8, w_down, w_d.at[0:hid])]

    sent, cleared = [], []

    def push(src, dst, target):
        i = len(sent)
        copy = pltpu.make_async_remote_copy(
            src_ref=src, dst_ref=dst, send_sem=ssem.at[i], recv_sem=rsem.at[i],
            device_id=target, device_id_type=pl.DeviceIdType.MESH)
        copy.start()
        sent.append(copy)
        return copy

    cuts = (pl.ds(0, META + quarter),) + tuple(pl.ds(META + c * quarter, quarter) for c in (1, 2, 3))
    parts = (slice(0, split), slice(split, width))
    spots = slice(0, META)
    quarters = [slice(c * quarter, (c + 1) * quarter) for c in range(4)]
    cut_q = [pl.ds(c * quarter, quarter) for c in range(4)]
    cut_h = [pl.ds(h * split, split) for h in range(2)]

    def forward(src, dst, target, c):
        return push(units.at[src, :, cuts[c]], units.at[dst, :, cuts[c]], target)

    pl.semaphore_wait(barrier, len(peers))
    chunks = (1, 0, 2, 3)
    a1, a2, a3, far = {}, {}, {}, {}

    def first(c):
        piece = tokens.at[:, cut_q[c]]
        a1[c] = (push(piece, units.at[1, :, cuts[c]], up), push(piece, units.at[2, :, cuts[c]], down))

    first(1)
    w_peer = [push(w_in.at[0], w_gu.at[:, hid:2 * hid], partner),
              push(w_in.at[1], w_gu.at[:, 3 * hid:4 * hid], partner),
              push(w_down, w_d.at[hid:2 * hid], partner)]
    for copy in small:
        copy.wait()
    units[0, :, spots] = routing_meta(old_s, new_s, ids_v[...], rep_v[...], comb_v[...])
    own.wait()
    a1[0] = (forward(0, 1, up, 0), forward(0, 2, down, 0))
    first(2)
    first(3)
    for c in chunks:
        a1[c][0].wait_recv()
        u = forward(1, 3, up, c)
        a1[c][1].wait_recv()
        a2[c] = (u, forward(2, 4, down, c))
    for c in chunks:
        a2[c][0].wait_recv()
        u = forward(3, 5, up, c)
        if c % 2 == 0:
            far[c] = forward(3, 7, up2, c)
        a2[c][1].wait_recv()
        a3[c] = (u, forward(4, 6, down, c))
        if c % 2 == 1:
            far[c] = forward(4, 7, down2, c)

    def wanted_by(n, block):
        return 32 * block + 8 * ((x + (n >> 4)) & (NX - 1)) + CAP * half + (n & 3)

    lane_i = lax.broadcasted_iota(jnp.int32, (META, 3 * META), 0)
    n_i = lax.broadcasted_iota(jnp.int32, (META, 3 * META), 1)
    n_in = n_i & (META - 1)
    spread = jnp.where((lane_i == wanted_by(n_in, n_i >> 7)) & (n_in < 64), 1.0, 0.0).astype(BF16)
    n_t = lax.broadcasted_iota(jnp.int32, (64, META), 0)
    spread_t = jnp.where(lax.broadcasted_iota(jnp.int32, (64, META), 1) == wanted_by(n_t, 3), 1.0, 0.0).astype(BF16)
    i_row = lax.broadcasted_iota(jnp.int32, (64, 64), 0)
    i_col = lax.broadcasted_iota(jnp.int32, (64, 64), 1)
    same_unit = (i_row >> 4) == ((i_col >> 2) & 3)
    same_unit_t = (i_col >> 4) == ((i_row >> 2) & 3)

    def weights_of(g):
        meta = units[4 * g:4 * g + 4, :, spots].reshape(64, META)
        picks = jnp.dot(meta, spread, preferred_element_type=F32)
        return jnp.concatenate(
            [jnp.where(same_unit, picks[:, q * META:q * META + 64], 0.0).astype(BF16) for q in range(3)], axis=0)

    def select(g, ready):
        copies = []
        for h in range(2):
            for copy in ready[h]:
                copy.wait_recv()
            if h == 0:
                meta = units[4 * g:4 * g + 4, :, spots].reshape(64, META)
                picks = lax.dot_general(spread_t, meta, (((1,), (1,)), ((), ())), preferred_element_type=F32)
                picks = jnp.where(same_unit_t, picks, 0.0).astype(BF16)
            for j in range(7):
                at = META + h * split + j * 256
                cut = slice(h * split + j * 256, h * split + (j + 1) * 256)
                group = units[4 * g:4 * g + 4, :, at:at + 256].reshape(64, 256)
                got = jnp.dot(picks, group, preferred_element_type=F32)
                got = got.astype(BF16)
                rows[g, 0, :, cut] = got[0:16]
                for d in range(1, NX):
                    sel[g, d, :, cut] = got[16 * d:16 * d + 16]
            copies.append({d: push(sel.at[g, d, :, cut_h[h]], rows.at[g, d, :, cut_h[h]], right[d])
                           for d in (2, 1, 3)})
        return copies

    def experts(g, copies, clear):
        gate_up = jnp.zeros((64, 4 * hid), F32)
        for h in range(2):
            for d in (1, 3, 2):
                copies[h][d].wait_recv()
            block = rows[g, :, :, parts[h]].reshape(64, split)
            gate_up = gate_up + jnp.dot(block, w_gu[parts[h], :], preferred_element_type=F32)
        gate = gate_up[:, :2 * hid]
        hidden = (gate * jax.nn.sigmoid(gate) * gate_up[:, 2 * hid:]).astype(BF16)
        back = []
        for h in range(2):
            for j in range(7):
                cut = slice(h * split + j * 256, h * split + (j + 1) * 256)
                value = jnp.dot(hidden, w_d[:, cut], preferred_element_type=F32).astype(BF16)
                r_recv[g, 0:16, cut] = value[0:16]
                r_send[g, 16:64, cut] = value[16:64]
            for d in (1, 2, 3):
                if clear is not None:
                    clear[h][d].wait_send()
                    cleared.append(clear[h][d])
            back.append([push(r_send.at[g, pl.ds(16 * d, 16), cut_h[h]], r_recv.at[g, pl.ds(16 * d, 16), cut_h[h]],
                              left[d]) for d in (2, 1, 3)])
        return back

    def mix(g, h, weights, copies):
        for copy in copies:
            copy.wait_recv()
        for j in range(7):
            cut = slice(h * split + j * 256, h * split + (j + 1) * 256)
            value = jnp.dot(weights, r_recv[g, :, cut], preferred_element_type=F32)
            value = value[0:64] + value[64:128] + value[128:192]
            part[4 * g:4 * g + 4, :, cut] = value.reshape(4, 16, 256)

    def hand(k, dst, c, target, *arrived):
        value = part[k, :, quarters[c]]
        for copy, buffer in arrived:
            copy.wait_recv()
            value = value + buffer[:, quarters[c]].astype(F32)
        y_send[k, :, quarters[c]] = value.astype(BF16)
        return push(y_send.at[k, :, cut_q[c]], dst.at[:, cut_q[c]], target)

    x_a = select(0, ((), ()))
    x_b = select(1, [[a3[c][0] for c in cs] + [a3[c][1] for c in cs] + [far[c] for c in cs]
                     for cs in ((1, 0), (2, 3))])
    for load in loads:
        load.wait()
    for copy in w_peer:
        copy.wait_recv()
    r_a = experts(0, x_a, x_b)
    r_b = experts(1, x_b, None)
    weights_a, weights_b = weights_of(0), weights_of(1)
    far_down, far_up, go_down, go_up = {}, {}, {}, {}
    for h in range(2):
        mix(1, h, weights_b, r_b[h])
        even, odd = 2 * h, 2 * h + 1
        far_down[even] = hand(7, y_far.at[0], even, down2)
        far_up[odd] = hand(7, y_far.at[1], odd, up2)
        for c in (odd, even):
            go_down[c] = hand(5, y_recv.at[3], c, down)
        for c in (even, odd):
            go_up[c] = hand(6, y_recv.at[4], c, up)
    for h in range(2):
        mix(0, h, weights_a, r_a[h])
    order = ((1, 0), (3, 2), (0, 1), (2, 3))
    for c_down, c_up in order:
        extra = ((far_down[c_down], y_far.at[0]),) if c_down in far_down else ()
        go_down[c_down] = hand(3, y_recv.at[1], c_down, down, (go_down[c_down], y_recv.at[3]), *extra)
        extra = ((far_up[c_up], y_far.at[1]),) if c_up in far_up else ()
        go_up[c_up] = hand(4, y_recv.at[2], c_up, up, (go_up[c_up], y_recv.at[4]), *extra)
    for c_down, c_up in order:
        go_down[c_down] = hand(1, y_recv.at[0], c_down, down, (go_down[c_down], y_recv.at[1]))
        go_up[c_up] = hand(2, y_recv.at[7], c_up, up, (go_up[c_up], y_recv.at[2]))
    done = []
    for c in (1, 3, 0, 2):
        go_down[c].wait_recv()
        go_up[c].wait_recv()
        value = (part[0, :, quarters[c]] + y_recv[0, :, quarters[c]].astype(F32)
                 + y_recv[7, :, quarters[c]].astype(F32))
        out_v[:, quarters[c]] = value.astype(BF16)
        done.append(local(9 + c, out_v.at[:, cut_q[c]], out.at[:, cut_q[c]]))
    for copy in sent:
        if not any(copy is other for other in cleared):
            copy.wait_send()
    for copy in done:
        copy.wait()


COPIES = 28 + 3 + 12 + 12 + 28


def body(tokens, w_in, w_down, old_place, new_place, expert_ids, replica, combine):
    count, width = tokens.shape
    hid = w_down.shape[0]
    hbm = pl.BlockSpec(memory_space=pl.ANY)
    return pl.pallas_call(
        kernel,
        out_shape=jax.ShapeDtypeStruct((count, width), BF16),
        in_specs=[pl.BlockSpec(memory_space=pltpu.MemorySpace.HBM)] * 8,
        out_specs=hbm,
        scratch_shapes=[
            pltpu.VMEM((8, count, META + width), BF16),
            pltpu.VMEM((2, NX, 16, width), BF16),
            pltpu.VMEM((2, NX, 16, width), BF16),
            pltpu.VMEM((width, 4 * hid), BF16),
            pltpu.VMEM((2 * hid, width), BF16),
            pltpu.VMEM((2, 64, width), BF16),
            pltpu.VMEM((2, 64, width), BF16),
            pltpu.VMEM((8, count, width), F32),
            pltpu.VMEM((8, count, width), BF16),
            pltpu.VMEM((8, count, width), BF16),
            pltpu.VMEM((2, count, width), BF16),
            pltpu.SMEM((SLOTS,), jnp.int32),
            pltpu.SMEM((SLOTS,), jnp.int32),
            pltpu.VMEM((2, count), jnp.int32),
            pltpu.VMEM((2, count), jnp.int32),
            pltpu.VMEM((2, count), F32),
            pltpu.VMEM((count, width), BF16),
            pltpu.SemaphoreType.DMA((COPIES,)),
            pltpu.SemaphoreType.DMA((COPIES,)),
            pltpu.SemaphoreType.DMA((13,)),
        ],
        compiler_params=pltpu.CompilerParams(
            collective_id=0, has_side_effects=True, vmem_limit_bytes=32 << 20),
    )(*[pltpu.with_memory_space_constraint(a, pltpu.MemorySpace.HBM) for a in (
        tokens, w_in, w_down, old_place, new_place, expert_ids.T, replica.T, combine.T)])


def solution(mesh):
    placed = (
        P(("group", "expert"), None),
        P(None, None, ("group", "expert")),
        P(("group", "expert"), None),
        P("group"),
        P("group"),
        P(("group", "expert"), None),
        P(("group", "expert"), None),
        P(("group", "expert"), None),
    )
    return jax.shard_map(
        body, mesh=mesh, in_specs=placed, out_specs=P(("group", "expert"), None), check_vma=False
    )
```

```python
import jax
import jax.numpy as jnp
from jax import lax
from jax.experimental import pallas as pl
from jax.experimental.pallas import tpu as pltpu
from jax.sharding import PartitionSpec as P

SLOTS = 8
CAP = 4
NX, NY = 4, 8
META = 128
TILE = 512
F32 = jnp.float32
BF16 = jnp.bfloat16


def routing_meta(old_place, new_place, expert_ids, replica, combine):
    rows = expert_ids.shape[1]
    diagonal = (lax.broadcasted_iota(jnp.int32, (rows, rows), 0)
                == lax.broadcasted_iota(jnp.int32, (rows, rows), 1))

    def column_of(array, k):
        return jnp.sum(jnp.where(diagonal, array[k:k + 1, :], 0), axis=1, keepdims=True)

    lane = lax.broadcasted_iota(jnp.int32, (1, META), 1)
    new_vec = jnp.full((1, META), -1, jnp.int32)
    old_vec = jnp.full((1, META), -1, jnp.int32)
    for t in range(SLOTS):
        new_vec = jnp.where(lane == t, new_place[t], new_vec)
        old_vec = jnp.where(lane == t, old_place[t], old_vec)
    count = jnp.zeros((1, META), jnp.int32)
    rank = jnp.zeros((1, META), jnp.int32)
    for t in range(SLOTS):
        same = jnp.where(new_vec == new_place[t], 1, 0)
        count = count + same
        rank = rank + jnp.where(lane > t, same, 0)
    source = jnp.where(new_vec == old_vec, lane, lane + 1 - 2 * (lane & 1))
    chosen = []
    for k in range(2):
        wanted = column_of(replica, k)
        wanted = jnp.where(wanted < count, wanted, wanted - count)
        hit = (new_vec == column_of(expert_ids, k)) & (rank == wanted)
        chosen.append(jnp.where(hit, 1.0, 0.0))
    row_i = lax.broadcasted_iota(jnp.int32, (rows, rows), 0)
    col_i = lax.broadcasted_iota(jnp.int32, (rows, rows), 1)
    earlier = jnp.where(col_i < row_i, 1.0, 0.0).astype(BF16)
    before = jnp.dot(earlier, (chosen[0] + chosen[1]).astype(BF16), preferred_element_type=F32)
    lanes = lax.broadcasted_iota(jnp.int32, (rows, META), 1)
    column = (lanes & 31).astype(F32)
    block = lanes >> 5
    source_f = (source * CAP).astype(F32)
    meta = jnp.zeros((rows, META), F32)
    for k in range(2):
        ahead = before if k == 0 else before + chosen[0]
        position = jnp.sum(chosen[k] * ahead, axis=1, keepdims=True)
        target = jnp.sum(chosen[k] * source_f, axis=1, keepdims=True) + position
        weight = column_of(combine, k)
        high = weight.astype(BF16).astype(F32)
        middle = (weight - high).astype(BF16).astype(F32)
        low = weight - high - middle
        value = jnp.where(block == 0, high, jnp.where(block == 1, middle, jnp.where(block == 2, low, 1.0)))
        meta = meta + jnp.where((column == target) & (position < float(CAP)), value, 0.0)
    return meta.astype(BF16)


def kernel(tokens, w_in, w_down, old_place, new_place, expert_ids, replica, combine, out,
           units, sel, rows, w_gu, w_d, r_send, r_recv, part, y_send, y_recv, y_far,
           old_s, new_s, ids_v, rep_v, comb_v, out_v, ssem, rsem, wsem):
    width = tokens.shape[1]
    hid = w_down.shape[0]
    me = lax.axis_index("expert")
    core = me % 2
    y = (me // 2) % NY
    x = me // (2 * NY)
    half = y // (NY // 2)

    def device(xx, yy, cc):
        return {"expert": (xx * NY + yy) * 2 + cc}

    up, up2 = device(x, (y + 1) % NY, core), device(x, (y + 2) % NY, core)
    down, down2 = device(x, (y + NY - 1) % NY, core), device(x, (y + NY - 2) % NY, core)
    partner = device(x, y, 1 - core)
    right = [device((x + d) % NX, y, core) for d in range(NX)]
    left = [device((x + NX - d) % NX, y, core) for d in range(NX)]

    barrier = pltpu.get_barrier_semaphore()
    peers = [up, down, up2, down2, partner] + right[1:]
    for peer in peers:
        pl.semaphore_signal(barrier, inc=1, device_id=peer, device_id_type=pl.DeviceIdType.MESH)

    split = width // 2
    quarter = width // 4

    def local(i, src, dst):
        copy = pltpu.make_async_copy(src, dst, wsem.at[i])
        copy.start()
        return copy

    small = [local(i, src, dst) for i, (src, dst) in enumerate((
        (old_place, old_s), (new_place, new_s), (expert_ids, ids_v), (replica, rep_v), (combine, comb_v)))]
    own = local(5, tokens, units.at[0, :, pl.ds(META, width)])
    loads = [local(6, w_in.at[0], w_gu.at[:, 0:hid]), local(7, w_in.at[1], w_gu.at[:, 2 * hid:3 * hid]),
             local(8, w_down, w_d.at[0:hid])]

    sent = []

    def push(src, dst, target):
        i = len(sent)
        copy = pltpu.make_async_remote_copy(
            src_ref=src, dst_ref=dst, send_sem=ssem.at[i], recv_sem=rsem.at[i],
            device_id=target, device_id_type=pl.DeviceIdType.MESH)
        copy.start()
        sent.append(copy)
        return copy

    cuts = (pl.ds(0, META + quarter),) + tuple(pl.ds(META + c * quarter, quarter) for c in (1, 2, 3))
    parts = (slice(0, split), slice(split, width))
    spots = slice(0, META)
    quarters = [slice(c * quarter, (c + 1) * quarter) for c in range(4)]
    cut_q = [pl.ds(c * quarter, quarter) for c in range(4)]
    cut_h = [pl.ds(h * split, split) for h in range(2)]

    def forward(src, dst, target, c):
        return push(units.at[src, :, cuts[c]], units.at[dst, :, cuts[c]], target)

    pl.semaphore_wait(barrier, len(peers))
    chunks = (1, 0, 2, 3)
    a1, a2, a3, far = {}, {}, {}, {}

    def first(c):
        piece = tokens.at[:, cut_q[c]]
        a1[c] = (push(piece, units.at[1, :, cuts[c]], up), push(piece, units.at[2, :, cuts[c]], down))

    first(1)
    w_peer = [push(w_in.at[0], w_gu.at[:, hid:2 * hid], partner),
              push(w_in.at[1], w_gu.at[:, 3 * hid:4 * hid], partner),
              push(w_down, w_d.at[hid:2 * hid], partner)]
    for copy in small:
        copy.wait()
    units[0, :, spots] = routing_meta(old_s, new_s, ids_v[...], rep_v[...], comb_v[...])
    own.wait()
    a1[0] = (forward(0, 1, up, 0), forward(0, 2, down, 0))
    first(2)
    first(3)
    for c in chunks:
        a1[c][0].wait_recv()
        u = forward(1, 3, up, c)
        a1[c][1].wait_recv()
        a2[c] = (u, forward(2, 4, down, c))
    for c in chunks:
        a2[c][0].wait_recv()
        u = forward(3, 5, up, c)
        if c % 2 == 0:
            far[c] = forward(3, 7, up2, c)
        a2[c][1].wait_recv()
        a3[c] = (u, forward(4, 6, down, c))
        if c % 2 == 1:
            far[c] = forward(4, 7, down2, c)

    def wanted_by(n, block):
        return 32 * block + 8 * ((x + (n >> 4)) & (NX - 1)) + CAP * half + (n & 3)

    lane_i = lax.broadcasted_iota(jnp.int32, (META, 3 * META), 0)
    n_i = lax.broadcasted_iota(jnp.int32, (META, 3 * META), 1)
    n_in = n_i & (META - 1)
    spread = jnp.where((lane_i == wanted_by(n_in, n_i >> 7)) & (n_in < 64), 1.0, 0.0).astype(BF16)
    n_t = lax.broadcasted_iota(jnp.int32, (64, META), 0)
    spread_t = jnp.where(lax.broadcasted_iota(jnp.int32, (64, META), 1) == wanted_by(n_t, 3), 1.0, 0.0).astype(BF16)
    i_row = lax.broadcasted_iota(jnp.int32, (64, 64), 0)
    i_col = lax.broadcasted_iota(jnp.int32, (64, 64), 1)
    same_unit = (i_row >> 4) == ((i_col >> 2) & 3)
    same_unit_t = (i_col >> 4) == ((i_row >> 2) & 3)

    def weights_of(g):
        meta = units[4 * g:4 * g + 4, :, spots].reshape(64, META)
        picks = jnp.dot(meta, spread, preferred_element_type=F32)
        return jnp.concatenate(
            [jnp.where(same_unit, picks[:, q * META:q * META + 64], 0.0).astype(BF16) for q in range(3)], axis=0)

    def select(g, ready):
        copies = []
        for h in range(2):
            for copy in ready[h]:
                copy.wait_recv()
            if h == 0:
                meta = units[4 * g:4 * g + 4, :, spots].reshape(64, META)
                picks = lax.dot_general(spread_t, meta, (((1,), (1,)), ((), ())), preferred_element_type=F32)
                picks = jnp.where(same_unit_t, picks, 0.0).astype(BF16)
            for j in range(7):
                at = META + h * split + j * 256
                cut = slice(h * split + j * 256, h * split + (j + 1) * 256)
                group = units[4 * g:4 * g + 4, :, at:at + 256].reshape(64, 256)
                got = jnp.dot(picks, group, preferred_element_type=F32)
                got = got.astype(BF16)
                rows[g, 0, :, cut] = got[0:16]
                for d in range(1, NX):
                    sel[g, d, :, cut] = got[16 * d:16 * d + 16]
            copies.append({d: push(sel.at[g, d, :, cut_h[h]], rows.at[g, d, :, cut_h[h]], right[d])
                           for d in (2, 1, 3)})
        return copies

    def give_back(g, h):
        return [push(r_send.at[g, pl.ds(16 * d, 16), cut_h[h]], r_recv.at[g, pl.ds(16 * d, 16), cut_h[h]], left[d])
                for d in (2, 1, 3)]

    def experts(g, copies, at_once):
        gate_up = jnp.zeros((64, 4 * hid), F32)
        for h in range(2):
            for d in (1, 3, 2):
                copies[h][d].wait_recv()
            block = rows[g, :, :, parts[h]].reshape(64, split)
            gate_up = gate_up + jnp.dot(block, w_gu[parts[h], :], preferred_element_type=F32)
        gate = gate_up[:, :2 * hid]
        hidden = (gate * jax.nn.sigmoid(gate) * gate_up[:, 2 * hid:]).astype(BF16)
        back = []
        for h in range(2):
            for j in range(7):
                cut = slice(h * split + j * 256, h * split + (j + 1) * 256)
                value = jnp.dot(hidden, w_d[:, cut], preferred_element_type=F32).astype(BF16)
                r_recv[g, 0:16, cut] = value[0:16]
                r_send[g, 16:64, cut] = value[16:64]
            if at_once:
                back.append(give_back(g, h))
        return back

    def mix(g, h, weights, copies):
        for copy in copies:
            copy.wait_recv()
        for j in range(7):
            cut = slice(h * split + j * 256, h * split + (j + 1) * 256)
            value = jnp.dot(weights, r_recv[g, :, cut], preferred_element_type=F32)
            value = value[0:64] + value[64:128] + value[128:192]
            part[4 * g:4 * g + 4, :, cut] = value.reshape(4, 16, 256)

    def hand(k, dst, c, target, *arrived):
        value = part[k, :, quarters[c]]
        for copy, buffer in arrived:
            copy.wait_recv()
            value = value + buffer[:, quarters[c]].astype(F32)
        y_send[k, :, quarters[c]] = value.astype(BF16)
        return push(y_send.at[k, :, cut_q[c]], dst.at[:, cut_q[c]], target)

    x_a = select(0, ((), ()))
    x_b = select(1, [[a3[c][0] for c in cs] + [a3[c][1] for c in cs] + [far[c] for c in cs]
                     for cs in ((1, 0), (2, 3))])
    for load in loads:
        load.wait()
    for copy in w_peer:
        copy.wait_recv()
    experts(0, x_a, False)
    r_b = experts(1, x_b, True)
    r_a = [give_back(0, h) for h in range(2)]
    weights_a, weights_b = weights_of(0), weights_of(1)
    far_down, far_up, go_down, go_up = {}, {}, {}, {}
    for h in range(2):
        mix(1, h, weights_b, r_b[h])
        even, odd = 2 * h, 2 * h + 1
        far_down[even] = hand(7, y_far.at[0], even, down2)
        far_up[odd] = hand(7, y_far.at[1], odd, up2)
        for c in (odd, even):
            go_down[c] = hand(5, y_recv.at[3], c, down)
        for c in (even, odd):
            go_up[c] = hand(6, y_recv.at[4], c, up)
    for h in range(2):
        mix(0, h, weights_a, r_a[h])
    order = ((1, 0), (3, 2), (0, 1), (2, 3))
    for c_down, c_up in order:
        extra = ((far_down[c_down], y_far.at[0]),) if c_down in far_down else ()
        go_down[c_down] = hand(3, y_recv.at[1], c_down, down, (go_down[c_down], y_recv.at[3]), *extra)
        extra = ((far_up[c_up], y_far.at[1]),) if c_up in far_up else ()
        go_up[c_up] = hand(4, y_recv.at[2], c_up, up, (go_up[c_up], y_recv.at[4]), *extra)
    for c_down, c_up in order:
        go_down[c_down] = hand(1, y_recv.at[0], c_down, down, (go_down[c_down], y_recv.at[1]))
        go_up[c_up] = hand(2, y_recv.at[7], c_up, up, (go_up[c_up], y_recv.at[2]))
    done = []
    for c in (1, 3, 0, 2):
        go_down[c].wait_recv()
        go_up[c].wait_recv()
        value = (part[0, :, quarters[c]] + y_recv[0, :, quarters[c]].astype(F32)
                 + y_recv[7, :, quarters[c]].astype(F32))
        out_v[:, quarters[c]] = value.astype(BF16)
        done.append(local(9 + c, out_v.at[:, cut_q[c]], out.at[:, cut_q[c]]))
    for copy in sent:
        copy.wait_send()
    for copy in done:
        copy.wait()


COPIES = 28 + 3 + 12 + 12 + 28


def body(tokens, w_in, w_down, old_place, new_place, expert_ids, replica, combine):
    count, width = tokens.shape
    hid = w_down.shape[0]
    hbm = pl.BlockSpec(memory_space=pl.ANY)
    return pl.pallas_call(
        kernel,
        out_shape=jax.ShapeDtypeStruct((count, width), BF16),
        in_specs=[pl.BlockSpec(memory_space=pltpu.MemorySpace.HBM)] * 8,
        out_specs=hbm,
        scratch_shapes=[
            pltpu.VMEM((8, count, META + width), BF16),
            pltpu.VMEM((2, NX, 16, width), BF16),
            pltpu.VMEM((2, NX, 16, width), BF16),
            pltpu.VMEM((width, 4 * hid), BF16),
            pltpu.VMEM((2 * hid, width), BF16),
            pltpu.VMEM((2, 64, width), BF16),
            pltpu.VMEM((2, 64, width), BF16),
            pltpu.VMEM((8, count, width), F32),
            pltpu.VMEM((8, count, width), BF16),
            pltpu.VMEM((8, count, width), BF16),
            pltpu.VMEM((2, count, width), BF16),
            pltpu.SMEM((SLOTS,), jnp.int32),
            pltpu.SMEM((SLOTS,), jnp.int32),
            pltpu.VMEM((2, count), jnp.int32),
            pltpu.VMEM((2, count), jnp.int32),
            pltpu.VMEM((2, count), F32),
            pltpu.VMEM((count, width), BF16),
            pltpu.SemaphoreType.DMA((COPIES,)),
            pltpu.SemaphoreType.DMA((COPIES,)),
            pltpu.SemaphoreType.DMA((13,)),
        ],
        compiler_params=pltpu.CompilerParams(
            collective_id=0, has_side_effects=True, vmem_limit_bytes=32 << 20),
    )(*[pltpu.with_memory_space_constraint(a, pltpu.MemorySpace.HBM) for a in (
        tokens, w_in, w_down, old_place, new_place, expert_ids.T, replica.T, combine.T)])


def solution(mesh):
    placed = (
        P(("group", "expert"), None),
        P(None, None, ("group", "expert")),
        P(("group", "expert"), None),
        P("group"),
        P("group"),
        P(("group", "expert"), None),
        P(("group", "expert"), None),
        P(("group", "expert"), None),
    )
    return jax.shard_map(
        body, mesh=mesh, in_specs=placed, out_specs=P(("group", "expert"), None), check_vma=False
    )
```
